32 devices in a mesh: parts: 2 (over x), chol: 16 (over z, y, core).
Axes of the slice: x: 2, y: 2, z: 4, core: 2. Of those that a mesh axis runs over, the one named last changes fastest.
Arguments:
- orbitals: float32 [32, 100, 1024], P(('parts', 'chol')), parts along dimension 0, may hold values from -6 to 6
- intersection_inv: float32 [32, 100, 100], P(('parts', 'chol')), parts along dimension 0, may hold values from -0.625 to 0.625
- factor_rows: bfloat16 [4096, 1024], P('chol'), may hold values from -0.1875 to 0.1875
- factor_rotated: bfloat16 [100, 4096], replicated, may hold values from -0.625 to 0.625
- factor_core: bfloat16 [1024, 4096], P('chol'), may hold values from -0.125 to 0.125
- fields: float32 [32, 1024], P('parts', 'chol'), parts along dimension 0, may hold values from -6 to 6
Outputs:
- propagated: float32 [32, 100, 1024], P(('parts', 'chol')), parts along dimension 0
- force_bias: float32 [32, 1024], P('parts', 'chol'), parts along dimension 0
The draws below stay inside these ranges and needn't reach their ends.
There are 2 independent parts, one for each index of `parts`. The reference program is written for one: setup_inputs(seed, part) draws one part's arguments, and reference() takes and returns one part's arrays. A program takes and returns all parts, laid end to end along the dimension named above; an argument that names none is the same for every part. Nothing has to cross between parts.
All inputs are finite; a program needn't handle non-finite values.
Results may differ from the reference program's by a relative error of at most 0.0091.
Values may be sent and summed in bfloat16 or wider, within the bound.
No kernel may reach another device: no remote copies, remote signals or barrier semaphores. Data moves between devices by JAX's collectives and lax.ppermute only.
A program may use at most 64 MiB of HBM per device.

```python
import jax
import jax.numpy as jnp
from jax import lax

M = 1024
NE = 100
NP = 4096
TAYLOR = 4
NCHOL = 1024
W = 16


def shard_levels(stream_key, dims, cuts, low, high):
    factor_of = 1.0
    for dim, blocks in cuts:
        draws = jax.random.uniform(jax.random.fold_in(jax.random.fold_in(stream_key, 6), dim), (blocks,), jnp.float32, low / len(cuts), high / len(cuts))
        factor_of = factor_of * jnp.repeat(jnp.exp(draws), dims[dim] // blocks).reshape((-1,) + (1,) * (len(dims) - 1 - dim))
    return factor_of


def normal_values(rng, dims, deviation, most, shards=(), held_as=jnp.bfloat16):
    level = shard_levels(rng, dims, shards, -0.22, 0.18) if shards else 1.0
    entries = jax.random.normal(rng, dims, jnp.float32) * deviation * level
    return jnp.minimum(jnp.maximum(entries, -most), most).astype(held_as)


def setup_inputs(seed: int = 0, part: int = 0) -> dict:
    keys = jax.random.split(jax.random.key(seed), 7)
    own_keys = jax.random.split(jax.random.fold_in(keys[6], part), 7)
    return {
        "orbitals": normal_values(own_keys[0], (W, NE, M), 1.0, 6.0, ((0, 16),), jnp.float32),
        "intersection_inv": normal_values(own_keys[1], (W, NE, NE), NE ** -0.5, 0.625, ((0, 16),), jnp.float32),
        "factor_rows": normal_values(keys[2], (NP, M), M ** -0.5, 0.1875, ((0, 16),)),
        "factor_rotated": normal_values(keys[3], (NE, NP), NE ** -0.5, 0.625),
        "factor_core": normal_values(keys[4], (NCHOL, NP), (NP * NCHOL // (2 * M)) ** -0.5, 0.125, ((0, 16),)),
        "fields": normal_values(own_keys[5], (W, NCHOL), 1.0, 6.0, ((1, 16),), jnp.float32),
    }


def density_one(half_green, factor_rows, factor_rotated):
    projected = lax.dot_general(half_green, factor_rows, (((1,), (1,)), ((), ())), preferred_element_type=jnp.float32)
    return jnp.sum(factor_rotated.astype(jnp.float32) * projected, axis=0).astype(jnp.bfloat16)


def propagate_one(orbital, potential, factor_rows):
    total = orbital
    term = orbital
    for order in range(1, TAYLOR + 1):
        summed = lax.dot_general(term.astype(jnp.bfloat16), factor_rows, (((1,), (1,)), ((), ())), preferred_element_type=jnp.float32)
        scaled = (summed * potential[None, :] / order).astype(jnp.bfloat16)
        term = jnp.dot(scaled, factor_rows, preferred_element_type=jnp.float32)
        total = total + term
    return total


def reference(orbitals, intersection_inv, factor_rows, factor_rotated, factor_core, fields):
    half_green = jnp.einsum("wij,wjm->wim", intersection_inv, orbitals, precision=lax.Precision.HIGHEST).astype(jnp.bfloat16)
    density = lax.map(lambda item: density_one(item, factor_rows, factor_rotated), half_green)
    force_bias = lax.dot_general(density, factor_core, (((1,), (1,)), ((), ())), preferred_element_type=jnp.float32)
    shifted = (fields - force_bias).astype(jnp.bfloat16)
    potential = jnp.dot(shifted, factor_core, preferred_element_type=jnp.float32)
    propagated = lax.map(lambda pair: propagate_one(pair[0], pair[1], factor_rows), (orbitals, potential))
    return propagated, force_bias
```

```python
import jax
import jax.numpy as jnp
from jax import lax
from jax.sharding import PartitionSpec as P

TAYLOR = 4


def density_one(half_green, all_rows, factor_rotated):
    projected = lax.dot_general(
        half_green, all_rows, (((1,), (1,)), ((), ())), preferred_element_type=jnp.float32
    )
    return jnp.sum(factor_rotated.astype(jnp.float32) * projected, axis=0).astype(jnp.bfloat16)


def propagate_one(orbital, potential, all_rows):
    total = orbital
    term = orbital
    for order in range(1, TAYLOR + 1):
        summed = lax.dot_general(
            term.astype(jnp.bfloat16),
            all_rows,
            (((1,), (1,)), ((), ())),
            preferred_element_type=jnp.float32,
        )
        scaled = (summed * potential[None, :] / order).astype(jnp.bfloat16)
        term = jnp.dot(scaled, all_rows, preferred_element_type=jnp.float32)
        total = total + term
    return total


def on_device(orbitals, intersection_inv, factor_rows, factor_rotated, factor_core, fields):
    walker_count = orbitals.shape[0]
    half_green = jnp.einsum(
        "wij,wjm->wim", intersection_inv, orbitals, precision=lax.Precision.HIGHEST
    ).astype(jnp.bfloat16)
    all_rows = lax.all_gather(factor_rows, "chol", axis=0, tiled=True)
    own_density = lax.map(lambda item: density_one(item, all_rows, factor_rotated), half_green)
    density = lax.all_gather(own_density, "chol", axis=0, tiled=True)
    force_bias = lax.dot_general(
        density, factor_core, (((1,), (1,)), ((), ())), preferred_element_type=jnp.float32
    )
    shifted = (fields - force_bias).astype(jnp.bfloat16)
    partial_sum = jnp.dot(shifted, factor_core, preferred_element_type=jnp.float32)
    partials = lax.all_to_all(
        partial_sum.reshape(-1, walker_count, partial_sum.shape[1]), "chol", 0, 0
    )
    potential = jnp.sum(partials, axis=0)
    propagated = lax.map(
        lambda pair: propagate_one(pair[0], pair[1], all_rows), (orbitals, potential)
    )
    return (propagated, force_bias)


def solution(mesh):
    in_specs = (
        P(("parts", "chol"), None, None),
        P(("parts", "chol"), None, None),
        P("chol", None),
        P(),
        P("chol", None),
        P("parts", "chol"),
    )
    out_specs = (P(("parts", "chol"), None, None), P("parts", "chol"))
    return jax.shard_map(
        on_device, mesh=mesh, in_specs=in_specs, out_specs=out_specs, check_vma=False
    )
```

```python
import jax
import jax.numpy as jnp
from jax import lax
from jax.experimental import pallas as pl
from jax.experimental.pallas import tpu as pltpu
from jax.sharding import PartitionSpec as P

TAYLOR = 4
LANES = 128
QUAD = 4
ANY = pl.BlockSpec(memory_space=pl.ANY)
VMEM = pl.BlockSpec(memory_space=pltpu.VMEM)
SMEM = pl.BlockSpec(memory_space=pltpu.SMEM)


def take_lanes(ref, offset, width):
    if width % LANES == 0:
        return ref[:, pl.ds(pl.multiple_of(offset, LANES), width)]
    base = pl.multiple_of(offset // LANES * LANES, LANES)
    shift = (LANES - offset % LANES) % LANES
    window = ref[:, pl.ds(base, LANES)].astype(jnp.float32)
    return pltpu.roll(window, shift, 1)[:, :width].astype(ref.dtype)


def add_lanes(ref, row, offset, value):
    width = value.shape[1]
    if width % LANES == 0:
        at = pl.ds(pl.multiple_of(offset, LANES), width)
        ref[row : row + 1, at] += value
        return
    base = pl.multiple_of(offset // LANES * LANES, LANES)
    padded = jnp.concatenate(
        [value, jnp.zeros((1, LANES - width), value.dtype)], axis=1
    )
    padded = jnp.broadcast_to(padded, (8, LANES))
    at = pl.ds(base, LANES)
    ref[row : row + 1, at] += pltpu.roll(padded, offset % LANES, 1)[:1]


def load_units(units, buffer, sems):
    rows = units[0].shape[0]
    copies = [
        pltpu.make_async_copy(unit, buffer.at[pl.ds(i * rows, rows)], sems.at[i])
        for i, unit in enumerate(units)
    ]
    for copy in copies:
        copy.start()
    return copies


def density_of(offsets, units, own_green, pair_green, factor_rotated, so_far):
    count = len(units)
    rows, basis = units[0].shape
    half = rows // 2
    points = factor_rotated.shape[1]

    def body(offsets_ref, *refs):
        unit_refs = refs[:count]
        rest = refs[count:]
        own_ref, pair_ref, rotated_ref, first_ref, out_ref, buffer, sems = rest
        copies = load_units(unit_refs, buffer, sems)
        out_ref[...] = first_ref[...]
        greens = [own_ref[...], pair_ref[...]]
        for i in range(count):
            copies[i].wait()
            values = buffer[i * rows : (i + 1) * rows, :]
            places = [offsets_ref[2 * i], offsets_ref[2 * i + 1]]
            rotated = [
                take_lanes(rotated_ref, place, half).astype(jnp.float32) for place in places
            ]
            for row, green in enumerate(greens):
                projected = lax.dot_general(
                    green, values, (((1,), (1,)), ((), ())), preferred_element_type=jnp.float32
                )
                for part in range(2):
                    piece = projected[:, part * half : (part + 1) * half]
                    summed = jnp.sum(piece * rotated[part], axis=0, keepdims=True)
                    add_lanes(out_ref, row, places[part], summed)

    return pl.pallas_call(
        body,
        out_shape=jax.ShapeDtypeStruct((2, points), jnp.float32),
        in_specs=[SMEM] + [ANY] * count + [VMEM] * 4,
        out_specs=VMEM,
        scratch_shapes=[
            pltpu.VMEM((count * rows, basis), units[0].dtype),
            pltpu.SemaphoreType.DMA((count,)),
        ],
        name="density",
    )(offsets, *units, own_green, pair_green, factor_rotated, so_far)


def bias_and_partials(place, densities, core, fields):
    count = len(densities)
    points = core.shape[1]
    vectors = core.shape[0]
    own = vectors // QUAD
    padded = max(8, count)

    def body(place_ref, *refs):
        density_refs = refs[:count]
        core_ref, fields_ref = refs[count : count + 2]
        outs = refs[count + 2 : -1]
        bias_refs, partial_refs = outs[:QUAD], outs[QUAD:]
        wide = refs[-1]
        z = place_ref[0]
        wide[...] = jnp.zeros_like(wide)
        for k in range(count):
            wide[pl.ds((z - k + count) % count, 1), :] = density_refs[k][...]
        core_all = core_ref[...]
        density = wide[...].astype(jnp.bfloat16)
        bias = lax.dot_general(
            density, core_all, (((1,), (1,)), ((), ())), preferred_element_type=jnp.float32
        )[:count]
        for q in range(QUAD):
            bias_refs[q][...] = bias[:, q * own : (q + 1) * own]
        shifted = (fields_ref[...] - bias).astype(jnp.bfloat16)
        wide[:count, :] = jnp.dot(shifted, core_all, preferred_element_type=jnp.float32)
        for k in range(count):
            partial_refs[k][...] = wide[pl.ds((z + k) % count, 1), :]

    outs = pl.pallas_call(
        body,
        out_shape=[jax.ShapeDtypeStruct((count, own), jnp.float32)] * QUAD
        + [jax.ShapeDtypeStruct((1, points), jnp.float32)] * count,
        in_specs=[SMEM] + [VMEM] * (count + 2),
        out_specs=[VMEM] * (QUAD + count),
        scratch_shapes=[pltpu.VMEM((padded, points), jnp.float32)],
        name="bias",
    )(place, *densities, core, fields)
    return outs[:QUAD], outs[QUAD:]


def propagate(offsets, units, partials, orbital):
    count = len(units)
    rows, basis = units[0].shape
    half = rows // 2
    points = count * rows
    electrons = orbital.shape[0]
    places = len(partials)
    chunk = min(points, 1024)
    step = chunk // rows
    wide = basis // 2

    def body(offsets_ref, *refs):
        unit_refs = refs[:count]
        partial_refs = refs[count : count + places]
        orbital_ref, out_ref, buffer, potential, ordered, acc, matrix, sems = refs[
            count + places :
        ]
        copies = load_units(unit_refs, buffer, sems)
        total = partial_refs[0][...]
        for ref in partial_refs[1:]:
            total = total + ref[...]
        potential[...] = total
        if half % LANES == 0:
            for i in range(2 * count):
                ordered[:, i * half : (i + 1) * half] = take_lanes(
                    potential, offsets_ref[i], half
                )
        else:
            per = LANES // half
            for i in range(2 * count // per):
                pieces = [
                    take_lanes(potential, offsets_ref[i * per + j], half) for j in range(per)
                ]
                ordered[:, i * LANES : (i + 1) * LANES] = jnp.concatenate(pieces, axis=1)
        for c in range(points // chunk):
            for i in range(c * step, (c + 1) * step):
                copies[i].wait()
            values = buffer[c * chunk : (c + 1) * chunk, :]
            weights = ordered[:, c * chunk : (c + 1) * chunk].reshape(chunk, 1)
            scaled = (values.astype(jnp.float32) * weights).astype(jnp.bfloat16)
            for j in range(2):
                cols = slice(j * wide, (j + 1) * wide)
                added = lax.dot_general(
                    scaled[:, : (j + 1) * wide],
                    values[:, cols],
                    (((0,), (0,)), ((), ())),
                    preferred_element_type=jnp.float32,
                )
                if c == 0:
                    acc[: (j + 1) * wide, cols] = added
                else:
                    acc[: (j + 1) * wide, cols] += added
        matrix[:, wide:] = acc[:, wide:].astype(jnp.bfloat16)
        matrix[:wide, :wide] = acc[:wide, :wide].astype(jnp.bfloat16)
        matrix[wide:, :wide] = matrix[:wide, wide:].T
        term = orbital_ref[...]
        result = term
        for order in range(1, TAYLOR + 1):
            term = jnp.dot(
                term.astype(jnp.bfloat16), matrix[...], preferred_element_type=jnp.float32
            ) * (1.0 / order)
            result = result + term
        out_ref[...] = result

    return pl.pallas_call(
        body,
        out_shape=jax.ShapeDtypeStruct((electrons, basis), jnp.float32),
        in_specs=[SMEM] + [ANY] * count + [VMEM] * (places + 1),
        out_specs=VMEM,
        scratch_shapes=[
            pltpu.VMEM((points, basis), units[0].dtype),
            pltpu.VMEM((1, points), jnp.float32),
            pltpu.VMEM((1, points), jnp.float32),
            pltpu.VMEM((basis, basis), jnp.float32),
            pltpu.VMEM((basis, basis), jnp.bfloat16),
            pltpu.SemaphoreType.DMA((count,)),
        ],
        compiler_params=pltpu.CompilerParams(vmem_limit_bytes=48 << 20),
        name="propagate",
    )(offsets, *units, *partials, orbital)


def on_device(parts, chol, orbitals, intersection_inv, factor_rows, factor_rotated, factor_core, fields):
    depth = chol // QUAD
    rows = factor_rows.shape[0]
    points = factor_rotated.shape[1]
    vectors = factor_core.shape[0]
    half = rows // 2
    me = lax.axis_index("chol")
    q, z = me % QUAD, me // QUAD
    h = lax.axis_index("parts") % 2

    def along_z(value, k):
        k = k % depth
        pairs = [(i, (i // QUAD + k) % depth * QUAD + i % QUAD) for i in range(chol)]
        return lax.ppermute(value, "chol", pairs)

    def across(value, bits):
        return lax.ppermute(value, "chol", [(i, i ^ bits) for i in range(chol)])

    def other_part(value):
        return lax.ppermute(value, "parts", [(i, i ^ 1) for i in range(parts)])

    own_half = lax.dynamic_slice_in_dim(factor_rows, h * half, half, 0)

    bases = [([(0, 0), (0, 1)], factor_rows)]
    received = []
    for k in range(1, depth // 2):
        a = jnp.concatenate([along_z(own_half, k), along_z(own_half, -k)], axis=0)
        received.append((k, a))
    y_own = across(factor_rows, 2)
    c_own = across(factor_rows, 1)
    half_green = jnp.einsum(
        "wij,wjm->wim", intersection_inv, orbitals, precision=lax.Precision.HIGHEST
    ).astype(jnp.bfloat16)[0]
    pair_green = across(half_green, 2)
    if received:
        own_half, y_own, *rest = lax.optimization_barrier(
            (own_half, y_own, *[a for _, a in received])
        )
        received = [(k, a) for (k, _), a in zip(received, rest)]
    last = along_z(own_half, depth // 2)
    core_y = across(factor_core, 2)
    core_c = across(factor_core, 1)
    for k, a in received:
        bases.append(([(-k, 2), (k, 2)], a))
        bases.append(([(-k, 3), (k, 3)], other_part(a)))
    last, core_y = lax.optimization_barrier((last, core_y))
    core_yc = across(core_y, 1)
    core = jnp.concatenate([factor_core, core_c, core_y, core_yc], axis=0)
    bases.append(
        (
            [(-(depth // 2), 2), (-(depth // 2), 3)],
            jnp.concatenate([last, other_part(last)], axis=0),
        )
    )

    def unit_offsets(where, bits):
        out = []
        for dz, part in where:
            side = [0, 1, h, 1 - h][part]
            owner = (z + dz + depth) % depth * QUAD + (q ^ bits)
            out.append(owner * rows + side * half)
        return out

    def offsets_of(units):
        return jnp.stack([o for where, bits, _ in units for o in unit_offsets(where, bits)]).astype(
            jnp.int32
        )

    near = []
    for where, unit in bases[:-1]:
        near.append((where, 0, unit))
        near.append((where, 1, c_own if unit is factor_rows else across(unit, 1)))
    late = [(bases[-1][0], 0, bases[-1][1]), (bases[-1][0], 1, across(bases[-1][1], 1))]

    def density_step(units, so_far):
        return density_of(
            offsets_of(units),
            [unit for _, _, unit in units],
            half_green,
            pair_green,
            factor_rotated,
            so_far,
        )

    density = density_step(near, jnp.zeros((2, points), jnp.float32))
    density = density_step(late, density)
    density = density[:1] + across(density[1:], 2)
    densities = [density] + [along_z(density, k) for k in range(1, depth)]

    by_quad = fields.reshape(depth, QUAD, vectors)

    def fields_for(bits):
        return lax.dynamic_index_in_dim(by_quad, q ^ bits, 1, keepdims=False)

    quad_fields = jnp.concatenate(
        [fields_for(0)] + [across(fields_for(bits), bits) for bits in range(1, QUAD)], axis=1
    )
    biases, partials = bias_and_partials(
        z.astype(jnp.int32).reshape(1), densities, core, quad_fields
    )
    sums = [partials[0]] + [along_z(partials[k], k) for k in range(1, depth)]

    far = []
    for where, unit in bases:
        y_unit = y_own if unit is factor_rows else across(unit, 2)
        far.append((where, 2, y_unit))
        far.append((where, 3, across(y_unit, 1)))
    units = near + late + far
    propagated = propagate(
        offsets_of(units), [unit for _, _, unit in units], sums, orbitals[0]
    )[None]

    shared = jnp.stack([biases[0]] + [across(biases[bits], bits) for bits in range(1, QUAD)])
    shared = jnp.stack(
        [lax.dynamic_index_in_dim(shared, q ^ bits, 0, keepdims=False) for bits in range(QUAD)],
        axis=1,
    )
    force_bias = shared.reshape(depth * QUAD, vectors)
    return (propagated, force_bias)


def solution(mesh):
    parts, chol = mesh.shape["parts"], mesh.shape["chol"]

    def step(*args):
        return on_device(parts, chol, *args)

    in_specs = (
        P(("parts", "chol"), None, None),
        P(("parts", "chol"), None, None),
        P("chol", None),
        P(),
        P("chol", None),
        P("parts", "chol"),
    )
    out_specs = (P(("parts", "chol"), None, None), P("parts", "chol"))
    return jax.shard_map(
        step, mesh=mesh, in_specs=in_specs, out_specs=out_specs, check_vma=False
    )
```

```python
import jax
import jax.numpy as jnp
from jax import lax
from jax.experimental import pallas as pl
from jax.experimental.pallas import tpu as pltpu
from jax.sharding import PartitionSpec as P


TAYLOR = 4
LANES = 128
QUAD = 4
ANY = pl.BlockSpec(memory_space=pl.ANY)
VMEM = pl.BlockSpec(memory_space=pltpu.VMEM)
SMEM = pl.BlockSpec(memory_space=pltpu.SMEM)


def take_lanes(ref, offset, width):
    if width % LANES == 0:
        return ref[:, pl.ds(pl.multiple_of(offset, LANES), width)]
    base = pl.multiple_of(offset // LANES * LANES, LANES)
    shift = (LANES - offset % LANES) % LANES
    window = ref[:, pl.ds(base, LANES)].astype(jnp.float32)
    return pltpu.roll(window, shift, 1)[:, :width].astype(ref.dtype)


def add_lanes(ref, row, offset, value):
    width = value.shape[1]
    if width % LANES == 0:
        at = pl.ds(pl.multiple_of(offset, LANES), width)
        ref[row : row + 1, at] += value
        return
    base = pl.multiple_of(offset // LANES * LANES, LANES)
    padded = jnp.concatenate(
        [value, jnp.zeros((1, LANES - width), value.dtype)], axis=1
    )
    padded = jnp.broadcast_to(padded, (8, LANES))
    at = pl.ds(base, LANES)
    ref[row : row + 1, at] += pltpu.roll(padded, offset % LANES, 1)[:1]


def start_copies(pairs, sems):
    copies = [
        pltpu.make_async_copy(source, target, sems.at[i])
        for i, (source, target) in enumerate(pairs)
    ]
    for copy in copies:
        copy.start()
    return copies


def row_blocks(refs, buffer):
    rows = refs[0].shape[0]
    return [(ref, buffer.at[pl.ds(i * rows, rows)]) for i, ref in enumerate(refs)]


def unit_offsets(unit, rows, depth):
    where, bits = unit
    me = lax.axis_index("chol")
    q, z = me % QUAD, me // QUAD
    h = lax.axis_index("parts") % 2
    out = []
    for dz, part in where:
        side = [0, 1, h, 1 - h][part]
        owner = (z + dz + depth) % depth * QUAD + other_member(q, bits)
        out.append(owner * rows + side * (rows // 2))
    return out


def other_member(q, bits):
    c = q % 2 if bits % 2 == 0 else 1 - q % 2
    y = q // 2 if bits // 2 == 0 else 1 - q // 2
    return y * 2 + c


def density_of(places, units, own_green, pair_green, factor_rotated, so_far, depth):
    count = len(units)
    rows, basis = units[0].shape
    half = rows // 2
    electrons, points = factor_rotated.shape
    first = so_far is None

    def body(*refs):
        unit_refs = refs[:count]
        rest = list(refs[count:])
        own_ref, pair_ref, rotated_hbm = rest[:3]
        del rest[:3]
        before = [] if first else [rest.pop(0) for _ in range(2)]
        own_out, pair_out, buffer, greens, rotated_ref, totals, sems = rest
        copies = start_copies(
            [(own_ref, greens.at[0]), (pair_ref, greens.at[1])]
            + row_blocks(unit_refs, buffer)
            + [(rotated_hbm, rotated_ref)]
            + [(ref, totals.at[pl.ds(i, 1)]) for i, ref in enumerate(before)],
            sems,
        )
        if first:
            totals[...] = jnp.zeros_like(totals)
        for i in (0, 1, *range(count + 2, len(copies))):
            copies[i].wait()
        for i in range(count):
            copies[i + 2].wait()
            values = buffer[i * rows : (i + 1) * rows, :]
            offsets = unit_offsets(places[i], rows, depth)
            rotated = [
                take_lanes(rotated_ref, offset, half).astype(jnp.float32) for offset in offsets
            ]
            for row in range(2):
                projected = lax.dot_general(
                    greens[row], values, (((1,), (1,)), ((), ())), preferred_element_type=jnp.float32
                )
                for part in range(2):
                    piece = projected[:, part * half : (part + 1) * half]
                    summed = jnp.sum(piece * rotated[part], axis=0, keepdims=True)
                    add_lanes(totals, row, offsets[part], summed)
        own_out[...] = totals[0:1, :]
        pair_out[...] = totals[1:2, :]

    extra = [] if first else list(so_far)
    return pl.pallas_call(
        body,
        out_shape=[jax.ShapeDtypeStruct((1, points), jnp.float32)] * 2,
        in_specs=[ANY] * (count + 3 + len(extra)),
        out_specs=[VMEM] * 2,
        scratch_shapes=[
            pltpu.VMEM((count * rows, basis), units[0].dtype),
            pltpu.VMEM((2, electrons, basis), own_green.dtype),
            pltpu.VMEM((electrons, points), factor_rotated.dtype),
            pltpu.VMEM((2, points), jnp.float32),
            pltpu.SemaphoreType.DMA((count + 3 + len(extra),)),
        ],
    )(*units, own_green, pair_green, factor_rotated, *extra)


def bias_and_partials(densities, cores, fields, depth):
    own, points = cores[0].shape
    vectors = own * QUAD
    padded = max(8, depth)

    def body(*refs):
        density_refs = refs[:depth]
        core_refs = refs[depth : depth + QUAD]
        fields_refs = refs[depth + QUAD : depth + 2 * QUAD]
        outs = refs[depth + 2 * QUAD : 2 * depth + 3 * QUAD]
        bias_refs, partial_refs = outs[:QUAD], outs[QUAD:]
        core, fields_in, wide, sems, out_sems = refs[2 * depth + 3 * QUAD :]
        z = lax.axis_index("chol") // QUAD
        wide[...] = jnp.zeros_like(wide)
        copies = start_copies(
            [
                (ref, wide.at[pl.ds((z - k + depth) % depth, 1)])
                for k, ref in enumerate(density_refs)
            ]
            + row_blocks(core_refs, core)
            + [(ref, fields_in.at[i]) for i, ref in enumerate(fields_refs)],
            sems,
        )
        for copy in copies:
            copy.wait()
        density = wide[...].astype(jnp.bfloat16)
        bias = lax.dot_general(
            density, core[...], (((1,), (1,)), ((), ())), preferred_element_type=jnp.float32
        )[:depth]
        fields_all = jnp.concatenate([fields_in[i] for i in range(QUAD)], axis=1)
        shifted = (fields_all - bias).astype(jnp.bfloat16)
        wide[:depth, :] = jnp.dot(shifted, core[...], preferred_element_type=jnp.float32)
        sends = start_copies(
            [(wide.at[pl.ds((z + k) % depth, 1)], ref) for k, ref in enumerate(partial_refs)],
            out_sems,
        )
        for i in range(QUAD):
            bias_refs[i][...] = bias[:, i * own : (i + 1) * own]
        for copy in sends:
            copy.wait()

    outs = pl.pallas_call(
        body,
        out_shape=[jax.ShapeDtypeStruct((depth, own), jnp.float32)] * QUAD
        + [jax.ShapeDtypeStruct((1, points), jnp.float32)] * depth,
        in_specs=[ANY] * (depth + 2 * QUAD),
        out_specs=[VMEM] * QUAD + [ANY] * depth,
        scratch_shapes=[
            pltpu.VMEM((vectors, points), cores[0].dtype),
            pltpu.VMEM((QUAD, depth, own), jnp.float32),
            pltpu.VMEM((padded, points), jnp.float32),
            pltpu.SemaphoreType.DMA((depth + 2 * QUAD,)),
            pltpu.SemaphoreType.DMA((depth,)),
        ],
        name="bias",
    )(*densities, *cores, *fields)
    return outs[:QUAD], outs[QUAD:]


def propagate(where, units, partials, orbital):
    count = len(units)
    rows, basis = units[0].shape
    half = rows // 2
    points = count * rows
    electrons = orbital.shape[0]
    places = len(partials)
    chunk = min(points, 1024)
    step = chunk // rows
    wide = basis // 2

    def body(*refs):
        unit_refs = refs[:count]
        partial_refs = refs[count : count + places]
        orbital_ref, out_ref, buffer, parts, potential, ordered, acc, matrix, sems = refs[
            count + places :
        ]
        small = start_copies(
            [(ref, parts.at[pl.ds(i, 1)]) for i, ref in enumerate(partial_refs)],
            sems.at[pl.ds(0, places)],
        )
        copies = start_copies(
            row_blocks(unit_refs, buffer), sems.at[pl.ds(places, count)]
        )
        for copy in small:
            copy.wait()
        potential[...] = jnp.sum(parts[...], axis=0, keepdims=True)
        offsets = [o for place in where for o in unit_offsets(place, rows, places)]
        per = max(1, LANES // half)
        for i in range(2 * count // per):
            pieces = [take_lanes(potential, offsets[i * per + j], half) for j in range(per)]
            piece = pieces[0] if per == 1 else jnp.concatenate(pieces, axis=1)
            ordered[:, i * half * per : (i + 1) * half * per] = piece
        for c in range(points // chunk):
            for i in range(c * step, (c + 1) * step):
                copies[i].wait()
            values = buffer[c * chunk : (c + 1) * chunk, :]
            weights = ordered[:, c * chunk : (c + 1) * chunk].reshape(chunk, 1)
            scaled = (values.astype(jnp.float32) * weights).astype(jnp.bfloat16)
            for j in range(2):
                cols = slice(j * wide, (j + 1) * wide)
                added = lax.dot_general(
                    scaled[:, : (j + 1) * wide],
                    values[:, cols],
                    (((0,), (0,)), ((), ())),
                    preferred_element_type=jnp.float32,
                )
                if c == 0:
                    acc[: (j + 1) * wide, cols] = added
                else:
                    acc[: (j + 1) * wide, cols] += added
        matrix[:, wide:] = acc[:, wide:].astype(jnp.bfloat16)
        matrix[:wide, :wide] = acc[:wide, :wide].astype(jnp.bfloat16)
        matrix[wide:, :wide] = matrix[:wide, wide:].T
        term = orbital_ref[...]
        result = term
        for order in range(1, TAYLOR + 1):
            term = jnp.dot(
                term.astype(jnp.bfloat16), matrix[...], preferred_element_type=jnp.float32
            ) * (1.0 / order)
            result = result + term
        out_ref[...] = result

    return pl.pallas_call(
        body,
        out_shape=jax.ShapeDtypeStruct((electrons, basis), jnp.float32),
        in_specs=[ANY] * (count + places) + [VMEM],
        out_specs=VMEM,
        scratch_shapes=[
            pltpu.VMEM((points, basis), units[0].dtype),
            pltpu.VMEM((places, points), jnp.float32),
            pltpu.VMEM((1, points), jnp.float32),
            pltpu.VMEM((1, points), jnp.float32),
            pltpu.VMEM((basis, basis), jnp.float32),
            pltpu.VMEM((basis, basis), jnp.bfloat16),
            pltpu.SemaphoreType.DMA((places + count,)),
        ],
        compiler_params=pltpu.CompilerParams(vmem_limit_bytes=48 << 20),
        name="propagate",
    )(*units, *partials, orbital)


def on_device(parts, chol, orbitals, intersection_inv, factor_rows, factor_rotated, factor_core, fields):
    depth = chol // QUAD
    rows = factor_rows.shape[0]
    vectors = factor_core.shape[0]
    half = rows // 2
    q = lax.axis_index("chol") % QUAD
    h = lax.axis_index("parts") % 2

    def along_z(value, k):
        k = k % depth
        pairs = [(i, (i // QUAD + k) % depth * QUAD + i % QUAD) for i in range(chol)]
        return lax.ppermute(value, "chol", pairs)

    def across(value, bits):
        return lax.ppermute(value, "chol", [(i, i ^ bits) for i in range(chol)])

    def other_part(value):
        return lax.ppermute(value, "parts", [(i, i ^ 1) for i in range(parts)])

    own_half = lax.dynamic_slice_in_dim(factor_rows, h * half, half, 0)
    whole = [(0, 0), (0, 1)]
    pairs = range(1, depth // 2)
    mid = depth // 2

    first = {k: (along_z(own_half, k), along_z(own_half, -k)) for k in pairs}
    half_green = jnp.einsum(
        "wij,wjm->wim", intersection_inv, orbitals, precision=lax.Precision.HIGHEST
    ).astype(jnp.bfloat16)[0]
    pair_green = across(half_green, 2)
    core_y = across(factor_core, 2)
    core_c = across(factor_core, 1)
    core_yc = across(core_y, 1)
    near = [(whole, 0, factor_rows), (whole, 1, across(factor_rows, 1))]
    ours = {k: jnp.concatenate(first[k], axis=0) for k in pairs}
    own_half, *rest = lax.optimization_barrier((own_half, *[ours[k] for k in pairs]))
    ours = dict(zip(pairs, rest))
    last = along_z(own_half, mid)
    theirs = {k: other_part(ours[k]) for k in pairs}
    for k in pairs:
        near.append(([(-k, 2), (k, 2)], 0, ours[k]))
        near.append(([(-k, 2), (k, 2)], 1, across(ours[k], 1)))
    for k in pairs:
        near.append(([(-k, 3), (k, 3)], 0, theirs[k]))
        near.append(([(-k, 3), (k, 3)], 1, across(theirs[k], 1)))
    final = jnp.concatenate([last, other_part(last)], axis=0)
    ends = [(-mid, 2), (-mid, 3)]
    late = [(ends, 0, final), (ends, 1, across(final, 1))]

    y_ours = {k: across(ours[k], 2) for k in pairs}
    y_last = across(last, 2)
    y_own = across(factor_rows, 2)
    y_theirs = {k: other_part(y_ours[k]) for k in pairs}
    y_final = jnp.concatenate([y_last, other_part(y_last)], axis=0)
    far = []
    for k in pairs:
        far.append(([(-k, 2), (k, 2)], 2, y_ours[k]))
        far.append(([(-k, 2), (k, 2)], 3, across(y_ours[k], 1)))
    far.append((whole, 2, y_own))
    far.append((whole, 3, across(y_own, 1)))
    for k in pairs:
        far.append(([(-k, 3), (k, 3)], 2, y_theirs[k]))
        far.append(([(-k, 3), (k, 3)], 3, across(y_theirs[k], 1)))
    far.append((ends, 2, y_final))
    far.append((ends, 3, across(y_final, 1)))

    def density_step(units, so_far):
        return density_of(
            [(where, bits) for where, bits, _ in units],
            [unit for _, _, unit in units],
            half_green,
            pair_green,
            factor_rotated,
            so_far,
            depth,
        )

    density = density_step(near, None)
    own_density, pair_density = density_step(late, density)
    density = own_density + across(pair_density, 2)
    densities = [density] + [along_z(density, k) for k in range(1, depth)]

    by_quad = fields.reshape(depth, QUAD, vectors)

    def member(array, bits, axis):
        return lax.dynamic_index_in_dim(array, other_member(q, bits), axis, keepdims=False)

    quad_fields = [member(by_quad, 0, 1)] + [
        across(member(by_quad, bits, 1), bits) for bits in range(1, QUAD)
    ]
    biases, partials = bias_and_partials(
        densities, [factor_core, core_c, core_y, core_yc], quad_fields, depth
    )
    sums = [partials[0]] + [along_z(partials[k], k) for k in range(1, depth)]

    units = near + late + far
    propagated = propagate(
        [(where, bits) for where, bits, _ in units],
        [unit for _, _, unit in units],
        sums,
        orbitals[0],
    )[None]

    shared = [biases[0]] + [across(biases[bits], bits) for bits in range(1, QUAD)]
    shared = jnp.stack(shared)
    shared = jnp.stack([member(shared, bits, 0) for bits in range(QUAD)], axis=1)
    return (propagated, shared.reshape(depth * QUAD, vectors))


def solution(mesh):
    parts, chol = mesh.shape["parts"], mesh.shape["chol"]

    def step(*args):
        return on_device(parts, chol, *args)

    in_specs = (
        P(("parts", "chol"), None, None),
        P(("parts", "chol"), None, None),
        P("chol", None),
        P(),
        P("chol", None),
        P("parts", "chol"),
    )
    out_specs = (P(("parts", "chol"), None, None), P("parts", "chol"))
    step = jax.shard_map(
        step, mesh=mesh, in_specs=in_specs, out_specs=out_specs, check_vma=False
    )
    return step
```
